32 devices in a mesh: gx: 4 (over z), gy: 8 (over y, x, core).
Axes of the slice: x: 2, y: 2, z: 4, core: 2. Of those that a mesh axis runs over, the one named last changes fastest.
Arguments:
- wind_u: float32 [16, 256, 512], P(None, 'gx', 'gy'), may hold values from -6 to 6
- wind_v: float32 [16, 256, 512], P(None, 'gx', 'gy'), may hold values from -6 to 6
- pressure: float32 [16, 256, 512], P(None, 'gx', 'gy'), may hold values from -6 to 6
- theta_field: float32 [16, 256, 512], P(None, 'gx', 'gy'), may hold values from -6 to 6
- vapor_field: float32 [16, 256, 512], P(None, 'gx', 'gy'), may hold values from -6 to 6
- sound_speed: float32 [16, 256, 512], P(None, 'gx', 'gy'), may hold values from 0.4 to 1.8
- fuel_kind: int32 [2560, 5120], P('gx', 'gy'), may hold values from 0 to 12
- burn_mask: int32 [2560, 5120], P('gx', 'gy'), may hold values 0 or 1
- level_gap: float32 [2560, 5120], P('gx', 'gy'), may hold values from 0.2 to 3
- base_rate: float32 [13], replicated, may hold values from 0.04 to 0.25
- wind_coef: float32 [13], replicated, may hold values from 0.05 to 0.3
- heat_yield: float32 [13], replicated, may hold values from 0.5 to 5
- vapor_yield: float32 [13], replicated, may hold values from 0.2 to 2
- send_tile: int32 [4, 8, 8, 2], P('gx', 'gy'), may hold values from -1 to 99, as said below
Outputs:
- east_wind: float32 [16, 256, 512], P(None, 'gx', 'gy')
- north_wind: float32 [16, 256, 512], P(None, 'gx', 'gy')
- new_pressure: float32 [16, 256, 512], P(None, 'gx', 'gy')
- new_theta: float32 [16, 256, 512], P(None, 'gx', 'gy')
- new_vapor: float32 [16, 256, 512], P(None, 'gx', 'gy')
- level_set: float32 [2560, 5120], P('gx', 'gy')
The draws below stay inside these ranges and needn't reach their ends.
Inputs may be any that keep to these rules, and one draw needn't show every extreme that they name: send_tile[a, b, o, c] is the index t of a burning tile of device (a, b) whose fire step device o of the gy axis in the same gx row computes, or -1 for an empty slot; no tile is named twice. Every device o is named by exactly 8 slots of its gy row in all; in every gy row one device burns 16 tiles, 2 for each owner; other devices burn 0 to 16 tiles.
All inputs are finite; a program needn't handle non-finite values. No bound on the sum of `burn_mask` on one device may be relied on, other than what follows from the above.
Results may differ from the reference program's by a relative error of at most 0.0003.
Values sent between devices are 32-bit elements; how exact they have to be, the bound alone decides.
No kernel may reach another device: no remote copies, remote signals or barrier semaphores. Data moves between devices by JAX's collectives and lax.ppermute only.
A program may use at most 128 MiB of HBM per device.

```python
import math
import jax
import jax.numpy as jnp
from jax import lax

LEVELS = 16
CX = 64
CY = 64
REFINE = 10
TILE = 64
ACOUSTIC = 4
FIRE_STEPS = 4
CAP = 2
NFUEL = 13
NX = 256
NY = 512
FIRE_X = 2560
FIRE_Y = 5120
TY = 10
TILES_DEV = 100
SLOTS = 16
OWNCAP = 8
N_GX = 4
N_GY = 8


def draw_send_tile(key, part):
    key_counts, key_order, key_tiles = jax.random.split(key, 3)
    half_count = N_GY // 2
    swings = jax.random.randint(key_counts, (N_GX, half_count), 0, OWNCAP + 1)
    swings = swings.at[:, 0].set(OWNCAP)
    deltas = jnp.concatenate([swings, -swings], axis=1)
    scores = jax.random.randint(key_order, (N_GX, N_GY), 0, 1024) * N_GY + jnp.arange(N_GY)[None, :]
    arrangement = jnp.argsort(scores, axis=1, stable=True)
    counts = OWNCAP + jnp.take_along_axis(deltas, arrangement, axis=1)
    starts = jnp.cumsum(counts, axis=1) - counts
    tile_scores = jax.random.randint(key_tiles, (N_GX, N_GY, TILES_DEV), 0, 4096) * TILES_DEV + jnp.arange(TILES_DEV)
    shuffled = jnp.argsort(tile_scores, axis=2, stable=True).astype(jnp.int32)
    owners = jnp.arange(N_GY)[None, None, :, None]
    slot_index = jnp.arange(CAP)[None, None, None, :]
    within = (owners - starts[:, :, None, None]) % N_GY + slot_index * N_GY
    listed = jnp.take_along_axis(shuffled, within.reshape(N_GX, N_GY, N_GY * CAP), axis=2)
    listed = listed.reshape(N_GX, N_GY, N_GY, CAP)
    return jnp.where(within < counts[:, :, None, None], listed, -1).astype(jnp.int32)


def plant(result, own_key, low, largest):
    index_at = [jax.random.randint(jax.random.fold_in(own_key, axis), (), 0, length) for axis, length in enumerate(result.shape)]
    longest = result.shape.index(max(result.shape))
    neighbour = index_at[:longest] + [(index_at[longest] + 1) % result.shape[longest]] + index_at[longest + 1:]
    return result.at[tuple(index_at)].set(low).at[tuple(neighbour)].set(largest)


def block_scale(own_key, shape, cuts, least, top_value):
    def one(dim, shards_of):
        draws = jax.random.uniform(jax.random.fold_in(jax.random.fold_in(own_key, 6), dim), (shards_of,), jnp.float32, least / len(cuts), top_value / len(cuts))
        return jnp.repeat(jnp.exp(draws), shape[dim] // shards_of).reshape((-1,) + (1,) * (len(shape) - dim - 1))

    loudness = one(*cuts[0])
    for cut in cuts[1:]:
        loudness = loudness * one(*cut)
    return loudness


def bell_draw(key, shape, spread, bound, pieces=(), kind=jnp.bfloat16):
    drawn = jax.random.normal(key, shape, jnp.float32) * spread
    if len(pieces) > 0:
        drawn = block_scale(key, shape, pieces, -0.22, 0.18) * drawn
    return jnp.clip(drawn, min=-bound, max=bound).astype(kind)


def setup_inputs(seed: int = 0) -> dict:
    streams_of = jax.random.split(jax.random.key(seed), 15)
    return {
        "wind_u": bell_draw(streams_of[0], (LEVELS, NX, NY), 1.0, 6.0, ((1, 4), (2, 8)), jnp.float32),
        "wind_v": bell_draw(streams_of[1], (LEVELS, NX, NY), 1.0, 6.0, ((1, 4), (2, 8)), jnp.float32),
        "pressure": bell_draw(streams_of[2], (LEVELS, NX, NY), 1.0, 6.0, ((1, 4), (2, 8)), jnp.float32),
        "theta_field": bell_draw(streams_of[3], (LEVELS, NX, NY), 1.0, 6.0, ((1, 4), (2, 8)), jnp.float32),
        "vapor_field": bell_draw(streams_of[4], (LEVELS, NX, NY), 1.0, 6.0, ((1, 4), (2, 8)), jnp.float32),
        "sound_speed": jnp.clip(jnp.exp(math.log(1.8) - 1.50407736 * jax.random.uniform(streams_of[5], (LEVELS, NX, NY), jnp.float32) ** block_scale(streams_of[5], (LEVELS, NX, NY), ((1, 4), (2, 8)), -0.2, 0.2)), 0.4, 1.8),
        "fuel_kind": plant(jax.random.randint(streams_of[6], (FIRE_X, FIRE_Y), 0, NFUEL), jax.random.fold_in(streams_of[6], 1), 0, NFUEL - 1).astype(jnp.int32),
        "burn_mask": plant((jax.random.randint(streams_of[7], (FIRE_X, FIRE_Y), 0, 2) < 1).astype(jnp.int32), jax.random.fold_in(streams_of[7], 1), 0, 1),
        "level_gap": jnp.clip(0.2 + 2.8 * jax.random.uniform(streams_of[8], (FIRE_X, FIRE_Y), jnp.float32) ** block_scale(streams_of[8], (FIRE_X, FIRE_Y), ((0, 4), (1, 8)), -0.2, 0.2), 0.2, 3.0),
        "base_rate": jnp.clip(jnp.exp(jax.random.uniform(streams_of[9], (NFUEL,), jnp.float32, math.log(0.04), math.log(0.25))), 0.04, 0.25),
        "wind_coef": jnp.clip(jnp.exp(jax.random.uniform(streams_of[10], (NFUEL,), jnp.float32, math.log(0.05), math.log(0.3))), 0.05, 0.3),
        "heat_yield": jnp.clip(jnp.exp(jax.random.uniform(streams_of[11], (NFUEL,), jnp.float32, math.log(0.5), math.log(5.0))), 0.5, 5.0),
        "vapor_yield": jnp.clip(jnp.exp(jax.random.uniform(streams_of[12], (NFUEL,), jnp.float32, math.log(0.2), math.log(2.0))), 0.2, 2.0),
        "send_tile": draw_send_tile(jax.random.fold_in(streams_of[14], 71), 0),
    }


acoustic_push = 1.0
surface_weight = 0.6
upper_weight = 0.4
slope_floor = 0.25
rate_limit = 0.45
front_width = 0.5
layer_decay = 0.5

def advance(level, base, along_east, along_north):
    centre = level[1:-1, 1:-1]
    back_x = centre - level[:-2, 1:-1]
    fore_x = level[2:, 1:-1] - centre
    back_y = centre - level[1:-1, :-2]
    fore_y = level[1:-1, 2:] - centre
    slope_x = 0.5 * (fore_x + back_x)
    slope_y = 0.5 * (fore_y + back_y)
    length = jnp.maximum(jnp.sqrt(slope_x * slope_x + slope_y * slope_y), slope_floor)
    facing = jnp.maximum((along_east * slope_x + along_north * slope_y) / length, 0.0)
    spread_rate = jnp.minimum(base + facing * jnp.sqrt(facing), rate_limit)
    upwind = jnp.sqrt(jnp.square(jnp.maximum(back_x, 0.0)) + jnp.square(jnp.minimum(fore_x, 0.0)) + jnp.square(jnp.maximum(back_y, 0.0)) + jnp.square(jnp.minimum(fore_y, 0.0)))
    return centre - spread_rate * upwind

def fire_tile(fields):
    level = fields[0]
    extent = fields.shape[1]
    for number in range(FIRE_STEPS):
        offset = number + 1
        trimmed = fields[1:, offset:extent - offset, offset:extent - offset]
        level = advance(level, trimmed[0], trimmed[1], trimmed[2])
    return level

def reference(wind_u, wind_v, pressure, theta_field, vapor_field, sound_speed, fuel_kind, burn_mask, level_gap, base_rate, wind_coef, heat_yield, vapor_yield, send_tile):
    eastward, northward, press_now = (wind_u, wind_v, pressure)
    for number in range(ACOUSTIC):
        east_new = eastward - acoustic_push * (0.5 * (jnp.roll(press_now, -1, 1) - jnp.roll(press_now, 1, 1)))
        north_new = northward - acoustic_push * (0.5 * (jnp.roll(press_now, -1, 2) - jnp.roll(press_now, 1, 2)))
        spread_out = 0.5 * (jnp.roll(east_new, -1, 1) - jnp.roll(east_new, 1, 1)) + 0.5 * (jnp.roll(north_new, -1, 2) - jnp.roll(north_new, 1, 2))
        press_now = press_now - sound_speed * spread_out
        eastward, northward = (east_new, north_new)
    surface_east = surface_weight * eastward[0] + upper_weight * eastward[1]
    surface_north = surface_weight * northward[0] + upper_weight * northward[1]
    level_start = jnp.where(burn_mask == 1, -level_gap, level_gap)
    flat_ids = send_tile.reshape(N_GX * N_GY * SLOTS).astype(jnp.int32)
    slot_iota = jnp.arange(N_GX * N_GY * SLOTS, dtype=jnp.int32)
    home_x = slot_iota // (N_GY * SLOTS)
    home_y = slot_iota // SLOTS % N_GY
    safe_ids = jnp.maximum(flat_ids, 0)
    row_start = (home_x * (CX * REFINE) + safe_ids // TY * TILE).astype(jnp.int32)
    col_start = (home_y * (CY * REFINE) + safe_ids % TY * TILE).astype(jnp.int32)
    extent = TILE + 2 * FIRE_STEPS
    reach = jnp.arange(extent, dtype=jnp.int32)

    def visit(level_out, item):
        listed, row_first, col_first = item
        rows_pick = (row_first - FIRE_STEPS + reach) % FIRE_X
        cols_pick = (col_first - FIRE_STEPS + reach) % FIRE_Y

        def patch(field):
            return jnp.take(jnp.take(field, rows_pick, axis=0), cols_pick, axis=1)
        kinds = patch(fuel_kind)
        level_tile = jnp.where(patch(burn_mask) == 1, -patch(level_gap), patch(level_gap))
        coef_tile = wind_coef[kinds]
        east_tile = jnp.take(jnp.take(surface_east, rows_pick // REFINE, axis=0), cols_pick // REFINE, axis=1)
        north_tile = jnp.take(jnp.take(surface_north, rows_pick // REFINE, axis=0), cols_pick // REFINE, axis=1)
        fields = jnp.stack([level_tile, base_rate[kinds], coef_tile * east_tile, coef_tile * north_tile])
        advanced = fire_tile(fields)
        before = lax.dynamic_slice(level_out, (row_first, col_first), (TILE, TILE))
        level_out = lax.dynamic_update_slice(level_out, jnp.where(listed, advanced, before), (row_first, col_first))
        return (level_out, None)
    level_set, unused = lax.scan(visit, level_start, (flat_ids >= 0, row_start, col_start))
    change = jax.nn.sigmoid(-level_set / front_width) - jax.nn.sigmoid(-level_start / front_width)
    heat_cols = (heat_yield[fuel_kind] * change).reshape(NX, REFINE, NY, REFINE).mean(axis=(1, 3))
    vapor_cols = (vapor_yield[fuel_kind] * change).reshape(NX, REFINE, NY, REFINE).mean(axis=(1, 3))
    profile = jnp.exp(-layer_decay * jnp.arange(LEVELS, dtype=jnp.float32))[:, None, None]
    return (eastward, northward, press_now, theta_field + profile * heat_cols, vapor_field + profile * vapor_cols, level_set)
```

```python
import functools
import math

import jax
import jax.numpy as jnp
from jax import lax
from jax.experimental import pallas as pl
from jax.experimental.pallas import tpu as pltpu
from jax.sharding import PartitionSpec as P

REFINE = 10
TILE = 64
ACOUSTIC = 4
FIRE_STEPS = 4
LANES = 128
HALO = 8
REACH = 4
GROUPS = 16

acoustic_push = 1.0
surface_weight = 0.6
upper_weight = 0.4
slope_floor = 0.25
rate_limit = 0.45
front_width = 0.5
layer_decay = 0.5
tiny = 1e-30

VMEM = pltpu.VMEM


def lane_iota(rows):
    return lax.broadcasted_iota(jnp.int32, (rows, LANES), 1)


def widen(block):
    return jnp.concatenate([block, jnp.zeros((block.shape[0], LANES - block.shape[1]), block.dtype)], axis=1)


def turn(block, shift, axis):
    size = block.shape[axis]
    return pltpu.roll(block, shift % size if isinstance(shift, int) else shift, axis)


def start_of(mask, gap):
    return jnp.where(mask == 1, -gap, gap)


def pack_kernel(u, v, p, c, fuel, mask, gap, to_low_x, to_high_x, to_low_y, to_high_y):
    levels, rows, cols = u.shape
    cells_x, cells_y = fuel.shape
    tiles = cells_y // LANES
    pairs = ((u, v), (p, c))
    for out, first in ((to_low_x, 0), (to_high_x, rows - HALO)):
        for number, (one, two) in enumerate(pairs):
            for level in range(levels):
                out[number * levels + level] = jnp.concatenate(
                    [one[level, first : first + HALO, :], two[level, first : first + HALO, :]], axis=1
                )
    for out, first, lead in ((to_low_x, 0, 0), (to_high_x, cells_x - HALO, HALO - REACH)):
        start = start_of(mask[first : first + HALO, :], gap[first : first + HALO, :])
        kinds = fuel[first : first + HALO, :].astype(jnp.float32)
        both = jnp.concatenate([start[lead : lead + REACH], kinds[lead : lead + REACH]], axis=0)
        for tile in range(tiles):
            out[2 * levels + tile] = both[:, tile * LANES : (tile + 1) * LANES]
    lane = lane_iota(rows)
    for number, field in enumerate((u, v, p, c)):
        low = jnp.zeros((rows, LANES), jnp.float32)
        high = jnp.zeros((rows, LANES), jnp.float32)
        for level in range(levels):
            moved = turn(widen(field[level]), HALO * level, 1)
            low = jnp.where((lane >> 3) == level, moved, low)
            high = jnp.where((((lane - (cols - HALO)) & (LANES - 1)) >> 3) == level, moved, high)
        to_low_y[number * rows : (number + 1) * rows, :] = low
        to_high_y[number * rows : (number + 1) * rows, :] = high
    depth = cells_x // GROUPS
    lane = lane_iota(depth)
    low = jnp.zeros((depth, LANES), jnp.float32)
    high = jnp.zeros((depth, LANES), jnp.float32)
    last = cells_y - LANES
    for group in range(GROUPS):
        here = slice(group * depth, (group + 1) * depth)
        start = start_of(mask[here, :LANES], gap[here, :LANES])
        kinds = fuel[here, :LANES].astype(jnp.float32)
        edge = jnp.where(lane < REACH, start, turn(kinds, REACH, 1))
        low = jnp.where((lane >> 3) == group, turn(edge, 8 * group, 1), low)
        start = start_of(mask[here, last:], gap[here, last:])
        kinds = fuel[here, last:].astype(jnp.float32)
        edge = jnp.where(lane >= LANES - REACH, start, turn(kinds, -REACH, 1))
        high = jnp.where((lane >> 3) == group, turn(edge, 8 * group + 8, 1), high)
    to_low_y[4 * rows :, :] = low
    to_high_y[4 * rows :, :] = high


def corner_kernel(levels, above, below, to_low, to_high):
    count = above.shape[0]
    lane = lane_iota(HALO)
    half = LANES // 2
    for side, source in enumerate((below, above)):
        for number in range(2):
            low = [jnp.zeros((HALO, LANES), jnp.float32) for _ in range(2)]
            high = [jnp.zeros((HALO, LANES), jnp.float32) for _ in range(2)]
            for level in range(levels):
                pair = source[number * levels + level]
                for part in range(2):
                    moved = turn(pair, HALO * level - half * part, 1)
                    low[part] = jnp.where((lane >> 3) == level, moved, low[part])
                    high[part] = jnp.where((((lane - (half - HALO)) & (LANES - 1)) >> 3) == level, moved, high[part])
            for part in range(2):
                to_low[(2 * number + part) * 2 + side] = low[part]
                to_high[(2 * number + part) * 2 + side] = high[part]
    first, last = 2 * levels, count - 1
    to_low[8] = jnp.where(lane < REACH, above[first], turn(below[first], REACH, 1))
    to_high[8] = jnp.where(lane >= LANES - REACH, above[last], turn(below[last], -REACH, 1))


def acoustic(u, v, p, c):
    for _ in range(ACOUSTIC):
        u = u - acoustic_push * (turn(p, -1, 0) - turn(p, 1, 0))
        v = v - acoustic_push * (turn(p, -1, 1) - turn(p, 1, 1))
        p = p - c * ((turn(u, -1, 0) - turn(u, 1, 0)) + (turn(v, -1, 1) - turn(v, 1, 1)))
    return u, v, p


def fire_step(level, base, east, north):
    up, down = turn(level, 1, 0), turn(level, -1, 0)
    left, right = turn(level, 1, 1), turn(level, -1, 1)
    dx, dy = down - up, right - left
    inverse = lax.rsqrt(jnp.maximum(dx * dx + dy * dy, 4.0 * slope_floor * slope_floor))
    facing = jnp.maximum((east * dx + north * dy) * inverse, 0.0)
    push = facing * facing * lax.rsqrt(jnp.maximum(facing, tiny))
    rate = jnp.minimum(base + push, rate_limit)
    ax = jnp.maximum(level - up, 0.0)
    bx = jnp.minimum(down - level, 0.0)
    ay = jnp.maximum(level - left, 0.0)
    by = jnp.minimum(right - level, 0.0)
    total = ax * ax + bx * bx + ay * ay + by * by
    return level - rate * (total * lax.rsqrt(jnp.maximum(total, tiny)))


def pick(table, index):
    return jnp.take_along_axis(table, index, axis=1, mode="promise_in_bounds")


def split(block):
    high = block.astype(jnp.bfloat16)
    return high, (block - high.astype(jnp.float32)).astype(jnp.bfloat16)


def exact_dot(left, right, dims):
    high, low = split(right)
    return lax.dot_general(left, high, dims, preferred_element_type=jnp.float32) + lax.dot_general(
        left, low, dims, preferred_element_type=jnp.float32
    )


def main_kernel(
    sends, u, v, p, c, theta, vapor, fuel, mask, gap, base_t, coef_t, heat_t, vapor_t,
    above, below, from_low, from_high, corner_low, corner_high,
    u_out, v_out, p_out, theta_out, vapor_out, level_out,
    level_ext, kind_ext, surface, east_rows, north_rows, pool_heat, pool_vapor, heat_sums, vapor_sums, col_index,
):
    levels, rows, cols = u.shape
    cells_x, cells_y = fuel.shape
    tiles_y = cells_y // TILE
    half = LANES // 2
    around = rows + 2 * HALO
    fields = (u, v, p, c)
    scales = (None, None, 0.5, 0.25)
    lane = lane_iota(around)

    def one_level(level, carry):
        shift = lax.rem(half - HALO * level + LANES, LANES)
        mine = (lane >> 3) == level
        loaded = []
        for number in range(4):
            pair, part = number // 2, number % 2
            low_rows = below[pair * levels + level]
            high_rows = above[pair * levels + level]
            if part:
                low_rows, high_rows = turn(low_rows, half, 1), turn(high_rows, half, 1)
            block = jnp.concatenate([widen(fields[number][level]), low_rows, high_rows], axis=0)
            here = slice(number * rows, (number + 1) * rows)
            right = jnp.concatenate([from_high[here, :], corner_high[2 * number], corner_high[2 * number + 1]], axis=0)
            left = jnp.concatenate([from_low[here, :], corner_low[2 * number], corner_low[2 * number + 1]], axis=0)
            sides = turn(jnp.where(mine, right, left), shift, 1)
            block = jnp.where(lane < cols, block, sides)
            if scales[number] is not None:
                block = block * scales[number]
            loaded.append(block)
        new_u, new_v, new_p = acoustic(*loaded)
        u_out[level] = new_u[:rows, :cols]
        v_out[level] = new_v[:rows, :cols]
        p_out[level] = 2.0 * new_p[:rows, :cols]

        @pl.when(level < 2)
        def _():
            surface[0, level] = new_u
            surface[1, level] = new_v

        return carry

    lax.fori_loop(0, levels, one_level, 0)

    for number, out in enumerate((east_rows, north_rows)):
        wind = surface_weight * surface[number, 0] + upper_weight * surface[number, 1]
        surface[number, 0] = wind
        out[:HALO, :] = jnp.broadcast_to(wind[around - 1 : around, :], (HALO, LANES))
        out[HALO + cells_x :, :] = jnp.broadcast_to(wind[rows : rows + 1, :], (HALO, LANES))
        for step in range(REFINE):
            out[pl.ds(HALO + step, rows, stride=REFINE), :] = wind[:rows, :]

    start = start_of(mask[...], gap[...])
    level_out[...] = start
    level_ext[HALO : HALO + cells_x, LANES : LANES + cells_y] = start
    kind_ext[HALO : HALO + cells_x, LANES : LANES + cells_y] = fuel[...]
    top, bottom = slice(0, HALO), slice(HALO + cells_x, 2 * HALO + cells_x)
    west, east = slice(0, LANES), slice(LANES + cells_y, 2 * LANES + cells_y)
    lane8 = lane_iota(HALO)
    low_half = lax.broadcasted_iota(jnp.int32, (HALO, LANES), 0) < REACH
    at_west, at_east = lane8 >= LANES - REACH, lane8 < REACH

    def put_rows(block, rows_to, cols_to, is_top, ok):
        swapped = turn(block, REACH, 0)
        level = swapped if is_top else block
        kind = block if is_top else swapped
        good = ~low_half if is_top else low_half
        if ok is not None:
            good = good & ok
        level_ext[rows_to, cols_to] = level
        kind_ext[rows_to, cols_to] = jnp.where(good, kind, 0.0).astype(jnp.int32)

    for tile in range(cells_y // LANES):
        cols_to = slice(LANES * (tile + 1), LANES * (tile + 2))
        put_rows(above[2 * levels + tile], top, cols_to, True, None)
        put_rows(below[2 * levels + tile], bottom, cols_to, False, None)
    put_rows(corner_low[8], top, west, True, at_west)
    put_rows(turn(corner_low[8], REACH, 1), bottom, west, False, at_west)
    put_rows(corner_high[8], top, east, True, at_east)
    put_rows(turn(corner_high[8], -REACH, 1), bottom, east, False, at_east)
    depth = cells_x // GROUPS
    lane_d = lane_iota(depth)
    for group in range(GROUPS):
        here = slice(HALO + group * depth, HALO + (group + 1) * depth)
        block = from_low[4 * rows :, :]
        level_ext[here, west] = turn(block, LANES - 8 - 8 * group, 1)
        kind = turn(block, LANES - REACH - 8 * group, 1)
        kind_ext[here, west] = jnp.where(lane_d >= LANES - REACH, kind, 0.0).astype(jnp.int32)
        block = from_high[4 * rows :, :]
        level_ext[here, east] = turn(block, -8 * group, 1)
        kind = turn(block, -8 * group - REACH, 1)
        kind_ext[here, east] = jnp.where(lane_d < REACH, kind, 0.0).astype(jnp.int32)

    slots = heat_sums.shape[0] // 8
    window = TILE + 2 * HALO
    lane_w = lane_iota(window)
    pool_heat[...] = jnp.zeros(pool_heat.shape, jnp.float32)
    pool_vapor[...] = jnp.zeros(pool_vapor.shape, jnp.float32)
    heat_sums[...] = jnp.zeros(heat_sums.shape, jnp.float32)
    vapor_sums[...] = jnp.zeros(vapor_sums.shape, jnp.float32)
    col_index[...] = jnp.zeros(col_index.shape, jnp.int32)
    base_b = jnp.broadcast_to(base_t[...], (window, LANES))
    coef_b = jnp.broadcast_to(coef_t[...], (window, LANES))
    heat_b = jnp.broadcast_to(heat_t[...], (TILE, LANES))
    vapor_b = jnp.broadcast_to(vapor_t[...], (TILE, LANES))
    lead = 2 * HALO
    caps = sends.shape[3]

    def one_tile(slot, carry):
        ident = sends[0, 0, slot // caps, lax.rem(slot, caps)]

        @pl.when(ident >= 0)
        def _():
            tile_x, tile_y = ident // tiles_y, lax.rem(ident, tiles_y)
            odd = lax.rem(tile_y, 2)
            first = pl.multiple_of(tile_x * TILE, TILE)
            own = pl.multiple_of((tile_y // 2 + 1) * LANES, LANES)
            other = pl.multiple_of((tile_y // 2 + 2 * odd) * LANES, LANES)
            beyond = ((1 - 2 * odd) * lane_w + jnp.where(odd == 1, 31, -96)) >= 0
            within = (lane_w + half * odd) & (LANES - 1)
            signed = jnp.where(within >= 96, within - LANES, within)
            column = jnp.floor((signed + tile_y * TILE).astype(jnp.float32) * (1.0 / REFINE) + 0.5 / REFINE)
            column = column.astype(jnp.int32) & (LANES - 1)

            def window_of(ref):
                return jnp.where(
                    beyond, ref[pl.ds(first, window), pl.ds(other, LANES)], ref[pl.ds(first, window), pl.ds(own, LANES)]
                )

            before = window_of(level_ext)
            kinds = window_of(kind_ext)
            base = pick(base_b, kinds)
            coef = pick(coef_b, kinds)
            push_east = coef * pick(east_rows[pl.ds(first, window), :], column)
            push_north = coef * pick(north_rows[pl.ds(first, window), :], column)
            level = before
            for _ in range(FIRE_STEPS):
                level = fire_step(level, base, push_east, push_north)
            inner = slice(HALO, HALO + TILE)
            level, before, kinds = level[inner], before[inner], kinds[inner]
            inside = within[inner] < TILE
            place = pl.ds(first, TILE), pl.ds(pl.multiple_of(own - LANES, LANES), LANES)
            level_out[place] = jnp.where(inside, level, level_out[place])
            change = jax.nn.sigmoid(level * (-1.0 / front_width)) - jax.nn.sigmoid(before * (-1.0 / front_width))
            change = jnp.where(inside, change, 0.0)
            pool_heat[lead : lead + TILE, :] = pick(heat_b, kinds) * change
            pool_vapor[lead : lead + TILE, :] = pick(vapor_b, kinds) * change
            offset = lax.rem(first, REFINE)
            rows_to = pl.ds(pl.multiple_of(slot * 8, 8), 8)
            for pool, sums in ((pool_heat, heat_sums), (pool_vapor, vapor_sums)):
                total = pool[pl.ds(lead - offset, 8, stride=REFINE), :]
                for step in range(1, REFINE):
                    total = total + pool[pl.ds(lead - offset + step, 8, stride=REFINE), :]
                sums[rows_to, :] = total
            col_index[rows_to, :] = column[:8]

        return carry

    lax.fori_loop(0, slots, one_tile, 0)

    row_of = jnp.full((rows, 8 * slots), -1, jnp.int32)
    wide = lax.broadcasted_iota(jnp.int32, (rows, 8 * slots), 1)
    heat_cols, vapor_cols = [], []
    to_cols = lax.broadcasted_iota(jnp.int32, (LANES, LANES), 0)
    transposed = (((1,), (1,)), ((), ()))
    for slot in range(slots):
        ident = jnp.maximum(sends[0, 0, slot // caps, slot % caps], 0)
        row_of = jnp.where((wide >> 3) == slot, (wide & 7) + (ident // tiles_y) * TILE // REFINE, row_of)
        here = slice(8 * slot, 8 * slot + 8)
        to_col = jnp.where(to_cols == jnp.broadcast_to(col_index[8 * slot : 8 * slot + 1, :], (LANES, LANES)), 1.0, 0.0)
        both = jnp.concatenate([heat_sums[here, :], vapor_sums[here, :]], axis=0)
        high, low = split(both)
        done = lax.dot_general(
            jnp.concatenate([high, low], axis=0), to_col.astype(jnp.bfloat16), transposed, preferred_element_type=jnp.float32
        )
        heat_cols.append(done[:8] + done[16:24])
        vapor_cols.append(done[8:16] + done[24:])
    to_row = jnp.where(row_of == lax.broadcasted_iota(jnp.int32, row_of.shape, 0), 1.0, 0.0).astype(jnp.bfloat16)
    plain = (((1,), (0,)), ((), ()))
    scale = 1.0 / (REFINE * REFINE)
    heat = (exact_dot(to_row, jnp.concatenate(heat_cols, axis=0), plain) * scale)[:, :cols]
    steam = (exact_dot(to_row, jnp.concatenate(vapor_cols, axis=0), plain) * scale)[:, :cols]
    for level in range(levels):
        factor = math.exp(-layer_decay * level)
        theta_out[level] = theta[level] + factor * heat
        vapor_out[level] = vapor[level] + factor * steam


def shifted(block, axis, step):
    count = lax.axis_size(axis)
    return lax.ppermute(block, axis, [(i, (i + step) % count) for i in range(count)])


def body(
    wind_u, wind_v, pressure, theta_field, vapor_field, sound_speed, fuel_kind, burn_mask, level_gap,
    base_rate, wind_coef, heat_yield, vapor_yield, send_tile,
):
    levels, rows, cols = wind_u.shape
    cells_x, cells_y = fuel_kind.shape
    f32 = jnp.float32
    vmem = pl.BlockSpec(memory_space=VMEM)
    smem = pl.BlockSpec(memory_space=pltpu.SMEM)
    params = pltpu.CompilerParams(vmem_limit_bytes=48 * 2**20)
    row_msg = jax.ShapeDtypeStruct((2 * levels + cells_y // LANES, HALO, LANES), f32)
    col_msg = jax.ShapeDtypeStruct((4 * rows + cells_x // GROUPS, LANES), f32)
    corner_msg = jax.ShapeDtypeStruct((9, HALO, LANES), f32)
    to_low_x, to_high_x, to_low_y, to_high_y = pl.pallas_call(
        pack_kernel,
        out_shape=(row_msg, row_msg, col_msg, col_msg),
        in_specs=[vmem] * 7,
        out_specs=[vmem] * 4,
        compiler_params=params,
        name="pack",
    )(wind_u, wind_v, pressure, sound_speed, fuel_kind, burn_mask, level_gap)
    above = shifted(to_high_x, "gx", 1)
    below = shifted(to_low_x, "gx", -1)
    from_low = shifted(to_high_y, "gy", 1)
    from_high = shifted(to_low_y, "gy", -1)
    corner_to_low, corner_to_high = pl.pallas_call(
        functools.partial(corner_kernel, levels),
        out_shape=(corner_msg, corner_msg),
        in_specs=[vmem] * 2,
        out_specs=[vmem] * 2,
        compiler_params=params,
        name="corners",
    )(above, below)
    corner_low = shifted(corner_to_high, "gy", 1)
    corner_high = shifted(corner_to_low, "gy", -1)

    def table(values):
        return jnp.pad(values, (0, LANES - values.shape[0])).reshape(1, LANES)

    slots = send_tile.shape[2] * send_tile.shape[3]
    around = rows + 2 * HALO
    extent = (cells_x + 2 * HALO, cells_y + 2 * LANES)
    atmosphere = jax.ShapeDtypeStruct(wind_u.shape, f32)
    return pl.pallas_call(
        main_kernel,
        out_shape=(atmosphere,) * 5 + (jax.ShapeDtypeStruct(level_gap.shape, f32),),
        in_specs=[smem] + [vmem] * 19,
        out_specs=[vmem] * 6,
        scratch_shapes=[
            VMEM(extent, f32),
            VMEM(extent, jnp.int32),
            VMEM((2, 2, around, LANES), f32),
            VMEM((extent[0], LANES), f32),
            VMEM((extent[0], LANES), f32),
            VMEM((TILE + 4 * HALO, LANES), f32),
            VMEM((TILE + 4 * HALO, LANES), f32),
            VMEM((8 * slots, LANES), f32),
            VMEM((8 * slots, LANES), f32),
            VMEM((8 * slots, LANES), jnp.int32),
        ],
        compiler_params=params,
        name="main",
    )(
        send_tile, wind_u, wind_v, pressure, sound_speed, theta_field, vapor_field, fuel_kind, burn_mask, level_gap,
        table(base_rate), table(wind_coef), table(heat_yield), table(vapor_yield),
        above, below, from_low, from_high, corner_low, corner_high,
    )


def solution(mesh):
    air = P(None, "gx", "gy")
    cells = P("gx", "gy")
    return jax.shard_map(
        body,
        mesh=mesh,
        in_specs=(air,) * 6 + (cells,) * 3 + (P(),) * 4 + (P("gx", "gy", None, None),),
        out_specs=(air,) * 5 + (cells,),
        check_vma=False,
    )
```
